512 devices in a mesh: blk: 128 (over z, x_lo, y), aux: 4 (over x_hi, core).
Axes of the slice: x: 4 (x_hi: 2, x_lo: 2; x = x_hi * 2 + x_lo), y: 8, z: 8, core: 2. Of those that a mesh axis runs over, the one named last changes fastest.
Arguments:
- ints3c: bfloat16 [8, 65536, 3, 512], P('aux', 'blk'), may hold values from -0.25 to 0.25
- coef: bfloat16 [65536, 256], P('blk'), may hold values from -6 to 6
- tile_mask: int32 [128, 3, 4], P('blk'), may hold values 0 or 1
Outputs:
- band: float32 [65536, 3, 512], P('blk', None, 'aux')
The draws below stay inside these ranges and needn't reach their ends.
All inputs are finite; a program needn't handle non-finite values. No bound on the sum of `tile_mask` on one device may be relied on, other than what follows from the above.
Results may differ from the reference program's by a relative error of at most 0.0016.
Values may be sent and summed in bfloat16 or wider, within the bound.
No kernel may reach another device: no remote copies, remote signals or barrier semaphores. Data moves between devices by JAX's collectives and lax.ppermute only.
A program may use at most 64 MiB of HBM per device.

```python
import jax
import jax.numpy as jnp
from jax import lax

BAS_DEV = 512
OCC_DEV = 256
TILES = 4
NBAS = 65536
NAUX = 8
N_BLK = 128


def place_ends(entries, stream_key, least, high):
    longest = entries.shape.index(max(entries.shape))
    spots = []
    for shift in (0, 1):
        where = [jax.random.randint(jax.random.fold_in(stream_key, axis), (), 0, length) for axis, length in enumerate(entries.shape)]
        where[longest] = (where[longest] + shift) % entries.shape[longest]
        spots.append(tuple(where))
    return entries.at[spots[0]].set(least).at[spots[1]].set(high)


def steps_of(rng, extent, pieces, least, largest):
    level = 1.0
    for position, parts in pieces:
        heights = jax.random.uniform(jax.random.fold_in(jax.random.fold_in(rng, 6), position), (parts,), jnp.float32, least / len(pieces), largest / len(pieces))
        level = level * jnp.repeat(jnp.exp(heights), extent[position] // parts).reshape((-1,) + (1,) * (len(extent) - 1 - position))
    return level


def noise(rng, extent, deviation, limit, pieces=(), held_as=jnp.bfloat16):
    drawn = jax.random.normal(rng, extent, jnp.float32) * deviation
    if len(pieces) > 0:
        drawn = steps_of(rng, extent, pieces, -0.22, 0.18) * drawn
    return jnp.clip(drawn, min=-limit, max=limit).astype(held_as)


def setup_inputs(seed: int = 0) -> dict:
    splits = jax.random.split(jax.random.key(seed), 4)
    return {
        "ints3c": noise(splits[0], (NAUX, NBAS, 3, BAS_DEV), BAS_DEV ** -0.5, 0.25, ((0, 4), (1, 128))),
        "coef": noise(splits[1], (NBAS, OCC_DEV), 1.0, 6.0, ((0, 128),)),
        "tile_mask": place_ends((jax.random.randint(splits[2], (N_BLK, 3, TILES), 0, 4) < 3).astype(jnp.int32), jax.random.fold_in(splits[2], 1), 0, 1),
    }


def reference(ints3c, coef, tile_mask):
    ints = jnp.moveaxis(ints3c.reshape(NAUX, N_BLK, BAS_DEV, 3, BAS_DEV), 1, 0)
    blocks = coef.reshape(N_BLK, BAS_DEV, OCC_DEV)
    windows = jnp.stack([jnp.roll(blocks, 1, 0), blocks, jnp.roll(blocks, -1, 0)], axis=1)
    weights = jnp.repeat(tile_mask.astype(jnp.float32), BAS_DEV // TILES, axis=2)

    def one_block(args):
        block_ints, block_coef, block_weights = args
        prod = jnp.einsum('pmkn,kni->pmki', block_ints.astype(jnp.float32), block_coef.astype(jnp.float32))
        return (prod * jnp.transpose(block_weights)[None, :, :, None]).astype(jnp.bfloat16)

    half = lax.map(one_block, (ints, windows, weights))
    scale = (NAUX * 3 * OCC_DEV) ** -0.5

    def band_block(index):
        own = half[index].astype(jnp.float32)
        after = half[(index + 1) % N_BLK].astype(jnp.float32)
        before = half[(index + N_BLK - 1) % N_BLK].astype(jnp.float32)
        diag = jnp.einsum('pmki,plki->ml', own, own)
        upper = jnp.einsum('pmki,plki->ml', own[:, :, 1:], after[:, :, :2])
        lower = jnp.einsum('pmki,plki->ml', own[:, :, :2], before[:, :, 1:])
        return jnp.stack([lower, diag, upper], axis=1) * scale

    band = lax.map(band_block, jnp.arange(N_BLK, dtype=jnp.int32))
    return band.reshape(NBAS, 3, BAS_DEV)
```

```python
import jax
import jax.numpy as jnp
from jax import lax
from jax.experimental import pallas as pl
from jax.experimental.pallas import tpu as pltpu
from jax.sharding import PartitionSpec as P

F32 = jnp.float32
BF16 = jnp.bfloat16
LIMIT = 8 << 20
MEDIUM = pl.CostEstimate(flops=3_000_000_000, bytes_accessed=1, transcendentals=0)
LARGE = pl.CostEstimate(flops=8_000_000_000, bytes_accessed=1, transcendentals=0)
SMALL = pl.CostEstimate(flops=1, bytes_accessed=1, transcendentals=0)


def dot_rows(left, right):
    return lax.dot_general(left, right, (((1,), (1,)), ((), ())), preferred_element_type=F32)


def weighted_half(mask_ref, k, plane, orbitals, out):
    tiles = mask_ref.shape[-1]
    step = out.shape[0] // tiles
    full = jnp.dot(plane[...], orbitals[...], preferred_element_type=F32)
    for t in range(tiles):
        spot = slice(t * step, (t + 1) * step)
        out[spot, :] = (full[spot] * mask_ref[k, 0, t].astype(F32)).astype(BF16)


def own_kernel(mask_ref, ints, orbitals, out, planes, held, sems):
    per = out.shape[0]
    first = pltpu.make_async_copy(orbitals, held, sems.at[per])
    copies = [
        pltpu.make_async_copy(ints.at[p, 1], planes.at[p], sems.at[p]) for p in range(per)
    ]
    for copy in [first] + copies:
        copy.start()
    first.wait()
    for p in range(per):
        copies[p].wait()
        weighted_half(mask_ref, 1, planes.at[p], held, out.at[p])


def own_middle(mask, ints, orbitals):
    per, _, rows, inner = ints.shape
    cols = orbitals.shape[1]
    hbm = pl.BlockSpec(memory_space=pltpu.HBM)
    return pl.pallas_call(
        own_kernel,
        in_specs=[pl.BlockSpec(memory_space=pltpu.SMEM), hbm, hbm],
        out_specs=pl.BlockSpec(memory_space=pltpu.VMEM),
        out_shape=jax.ShapeDtypeStruct((per, rows, cols), BF16),
        scratch_shapes=[
            pltpu.VMEM((per, rows, inner), BF16),
            pltpu.VMEM((inner, cols), BF16),
            pltpu.SemaphoreType.DMA((per + 1,)),
        ],
        compiler_params=pltpu.CompilerParams(vmem_limit_bytes=LIMIT),
        cost_estimate=SMALL,
        name="own_middle",
    )(mask, ints, orbitals)


def mate_kernel(mask_ref, ints, orbitals, out):
    for p in range(out.shape[0]):
        weighted_half(mask_ref, 1, ints.at[p, 1], orbitals, out.at[p])


def edge_kernel(mask_ref, place_ref, own, mate, orbitals, out, planes, sems):
    side = 2 - 2 * place_ref[0]
    per = planes.shape[0]
    copies = [
        pltpu.make_async_copy(own.at[p, side], planes.at[p], sems.at[p]) for p in range(per)
    ]
    for copy in copies:
        copy.start()
    for p in range(per):
        weighted_half(mask_ref, side, mate.at[p, side], orbitals, out.at[per + p])
    for p in range(per):
        copies[p].wait()
        weighted_half(mask_ref, side, planes.at[p], orbitals, out.at[p])


def edge_half(mask, place, own, mate, orbitals):
    per, _, rows, inner = own.shape
    cols = orbitals.shape[1]
    smem = pl.BlockSpec(memory_space=pltpu.SMEM)
    vmem = pl.BlockSpec(memory_space=pltpu.VMEM)
    return pl.pallas_call(
        edge_kernel,
        in_specs=[smem, smem, pl.BlockSpec(memory_space=pltpu.HBM), vmem, vmem],
        out_specs=vmem,
        out_shape=jax.ShapeDtypeStruct((2 * per, rows, cols), BF16),
        scratch_shapes=[
            pltpu.VMEM((per, rows, inner), BF16),
            pltpu.SemaphoreType.DMA((per,)),
        ],
        compiler_params=pltpu.CompilerParams(vmem_limit_bytes=LIMIT),
        cost_estimate=MEDIUM,
        name="edge_half",
    )(mask, place, own, mate, orbitals)


def diag_kernel(place_ref, edge, own, kept, sent):
    core = place_ref[0]
    rows = edge.shape[1]
    mid = rows // 2
    quarter = mid // 2
    for h in range(2):
        spot = pl.ds(h * mid, mid)
        for r in range(2):
            band = pl.ds(r * mid, mid)
            total = dot_rows(edge[0, band, :], edge[0, spot, :])
            for p in range(1, edge.shape[0]):
                total += dot_rows(edge[p, band, :], edge[p, spot, :])
            for p in range(own.shape[0]):
                total += dot_rows(own[p, band, :], own[p, spot, :])
            first, second = total[:, :quarter], total[:, quarter:]
            kept[h, band, :] = jnp.where(core == 0, first, second)
            sent[h, band, :] = jnp.where(core == 0, second, first)


def near_kernel(edge, near, same, out):
    rows = edge.shape[1]
    per = near.shape[0]
    mid = rows // 2
    for r in range(2):
        band = pl.ds(r * mid, mid)
        total = dot_rows(edge[0, band, :], same[0])
        for p in range(1, per):
            total += dot_rows(edge[p, band, :], same[p])
        for p in range(per):
            total += dot_rows(edge[per + p, band, :], near[p])
        out[band, :] = total


def last_kernel(place_ref, part, own, mate, other, kept, got, mine, theirs):
    far = place_ref[1]
    rows = own.shape[1]
    per = own.shape[0]
    mid = rows // 2
    for r in range(2):
        band = pl.ds(r * mid, mid)
        total = part[band, :]
        for p in range(per):
            total += dot_rows(own[p, band, :], other[per + p])
        for p in range(per):
            total += dot_rows(mate[p, band, :], other[p])
        first, second = total[:, :mid], total[:, mid:]
        mine[band, :mid] = jnp.where(far == 0, first, second)
        theirs[band, :mid] = jnp.where(far == 0, second, first).astype(BF16)
        mine[band, mid:] = kept[far, band, :] + got[far, band, :]
        theirs[band, mid:] = (kept[1 - far, band, :] + got[1 - far, band, :]).astype(BF16)


def whole(kernel, name, outs, *operands, scalars=0, cost=SMALL):
    smem = pl.BlockSpec(memory_space=pltpu.SMEM)
    vmem = pl.BlockSpec(memory_space=pltpu.VMEM)
    return pl.pallas_call(
        kernel,
        in_specs=[smem] * scalars + [vmem] * (len(operands) - scalars),
        out_specs=[vmem] * len(outs),
        out_shape=outs,
        compiler_params=pltpu.CompilerParams(vmem_limit_bytes=LIMIT),
        cost_estimate=cost,
        name=name,
    )(*operands)


def body(ints3c, coef, tile_mask):
    blocks = lax.axis_size("blk")
    group = lax.axis_size("aux")
    aux = lax.axis_index("aux")
    core = aux % 2
    far = aux // 2
    place = jnp.stack([core, far])
    mask = jnp.transpose(tile_mask, (1, 0, 2))

    def device(b, a):
        return (b % blocks) * group + a

    members = [(b, a) for b in range(blocks) for a in range(group)]

    def moved(value, target):
        pairs = [(device(b, a), target(b, a)) for b, a in members]
        return lax.ppermute(value, ("blk", "aux"), pairs)

    def to_edge(value):
        return moved(value, lambda b, a: device(b + 1 - 2 * (a % 2), a ^ 1))

    def to_same(value):
        return moved(value, lambda b, a: device(b - 1 + 2 * (a % 2), a))

    def to_mate(value):
        return moved(value, lambda b, a: device(b, a ^ 1))

    def to_far(value):
        return moved(value, lambda b, a: device(b, a ^ 2))

    def pick(index, first, second):
        return jnp.where(index == 0, first, second)

    ints = jnp.transpose(ints3c, (0, 2, 1, 3))
    per, _, rows, _ = ints.shape
    own_half = own_middle(mask, ints, coef)
    ints, coef, own_half = lax.optimization_barrier((ints, coef, own_half))
    edge_coef = to_edge(coef)
    mate_ints = to_mate(ints)
    near = to_edge(own_half)
    same = to_same(own_half)
    edges = edge_half(mask, place, ints, mate_ints, edge_coef)
    other = to_edge(edges)
    (mate_half,) = whole(
        mate_kernel,
        "mate_middle",
        [jax.ShapeDtypeStruct(own_half.shape, BF16)],
        mask,
        mate_ints,
        coef,
        scalars=1,
    )

    quarter = rows // group
    split = jax.ShapeDtypeStruct((2, rows, quarter), F32)
    kept, sent = whole(
        diag_kernel, "diag", [split, split], place, edges, own_half, scalars=1
    )
    got = to_mate(sent)

    full = jax.ShapeDtypeStruct((rows, rows), F32)
    (part,) = whole(near_kernel, "near", [full], edges, near, same, cost=LARGE)
    width = rows // 2 + quarter
    mine, theirs = whole(
        last_kernel,
        "last",
        [jax.ShapeDtypeStruct((rows, width), F32), jax.ShapeDtypeStruct((rows, width), BF16)],
        place,
        part,
        own_half,
        mate_half,
        other,
        kept,
        got,
        scalars=1,
    )
    scale = (group * per * 3 * own_half.shape[2]) ** (-0.5)
    total = (mine + to_far(theirs).astype(F32)) * scale
    left, right, diag = (total[:, i * quarter : (i + 1) * quarter] for i in range(3))
    kept = pick(core, left, right)
    got = to_mate(pick(core, right, left))
    return jnp.stack([pick(core, got, kept), diag, pick(core, kept, got)], axis=1)


def solution(mesh):
    placed = (P("aux", "blk", None, None), P("blk", None), P("blk", None, None))
    return jax.shard_map(
        body, mesh=mesh, in_specs=placed, out_specs=P("blk", None, "aux"), check_vma=False
    )
```

```python
import jax
import jax.numpy as jnp
from jax import lax
from jax.experimental import pallas as pl
from jax.experimental.pallas import tpu as pltpu
from jax.sharding import PartitionSpec as P

F32 = jnp.float32
BF16 = jnp.bfloat16
LIMIT = 8 << 20
SMEM = pl.BlockSpec(memory_space=pltpu.SMEM)
VMEM = pl.BlockSpec(memory_space=pltpu.VMEM)
HBM = pl.BlockSpec(memory_space=pltpu.HBM)


def call(kernel, name, specs, outs, operands, scratch=(), cost=1, out_specs=None, aliases=None):
    return pl.pallas_call(
        kernel,
        in_specs=specs,
        out_specs=[VMEM] * len(outs) if out_specs is None else out_specs,
        out_shape=outs,
        scratch_shapes=scratch,
        input_output_aliases=aliases or {},
        compiler_params=pltpu.CompilerParams(vmem_limit_bytes=LIMIT),
        cost_estimate=pl.CostEstimate(flops=int(cost), bytes_accessed=1, transcendentals=0),
        name=name,
    )(*operands)


def in_hbm(value):
    return pltpu.with_memory_space_constraint(value, pltpu.HBM)


def dot_rows(left, right):
    return lax.dot_general(left, right, (((1,), (1,)), ((), ())), preferred_element_type=F32)


def weighted(mask_ref, k, first, plane, orbitals):
    full = jnp.dot(plane[...], orbitals[...], preferred_element_type=F32)
    step = 128
    tiles = [
        full[t * step : (t + 1) * step] * mask_ref[k, 0, first + t].astype(F32)
        for t in range(full.shape[0] // step)
    ]
    return jnp.concatenate(tiles, axis=0).astype(BF16)


def sides():
    aux = lax.axis_index("aux")
    return lax.rem(aux, 2), lax.div(aux, 2)


def own_kernel(mask, ints, orbitals, out, held, mask_ref, planes, sems):
    per = out.shape[0]
    copies = [
        pltpu.make_async_copy(ints.at[p, 1], planes.at[p], sems.at[p]) for p in range(per)
    ]
    copies.append(pltpu.make_async_copy(orbitals, held, sems.at[per]))
    copies.append(pltpu.make_async_copy(mask, mask_ref, sems.at[per + 1]))
    for i in (per, 0, per + 1, *range(1, per)):
        copies[i].start()
    copies[per].wait()
    copies[per + 1].wait()
    for p in range(per):
        copies[p].wait()
        out[p] = weighted(mask_ref, 1, 0, planes.at[p], held)


def mate_kernel(mask, ints, orbitals, out, mask_ref, planes, sems):
    per = out.shape[0]
    copies = [
        pltpu.make_async_copy(ints.at[p, 1], planes.at[p], sems.at[p]) for p in range(per)
    ]
    copies.append(pltpu.make_async_copy(mask, mask_ref, sems.at[per]))
    for copy in copies:
        copy.start()
    copies[per].wait()
    for p in range(per):
        copies[p].wait()
        out[p] = weighted(mask_ref, 1, 0, planes.at[p], orbitals)


def spot(part, size):
    return pl.ds(pl.multiple_of(part * size, size), size)


def edge_kernel(mask, own, mate, orbitals, away, home, mask_ref, planes, sems):
    core, far = sides()
    side = 2 - 2 * core
    count, rows, _ = planes.shape
    per = count // 2
    mid = rows // 2
    copies = []
    for p in range(count):
        source = own.at[p, side] if p < per else mate.at[p - per, side]
        copies.append(pltpu.make_async_copy(source, planes.at[p], sems.at[p]))
    copies.append(pltpu.make_async_copy(mask, mask_ref, sems.at[count]))
    for copy in copies:
        copy.start()
    copies[count].wait()
    for p in range(count):
        copies[p].wait()
        for out, part in ((away, 1 - far), (home, far)):
            plane = planes.at[p, spot(part, mid)]
            out[p] = weighted(mask_ref, side, 2 * part, plane, orbitals)


def product(left, right):
    total = dot_rows(left[0][...], right[0][...])
    for i in range(1, len(left)):
        total += dot_rows(left[i][...], right[i][...])
    return total


def planes_of(ref, count, rows):
    return [ref.at[p, rows] for p in range(count)]


def diag_kernel(away, home, own, kept, sent):
    core, far = sides()
    count, mid, _ = away.shape
    per = own.shape[0]
    quarter = mid // 2
    every = pl.ds(0, mid)
    parts = ((1 - far, away), (far, home))
    for part, right in parts:
        rights = planes_of(right, count, every) + planes_of(own, per, spot(part, mid))
        for band, left in parts:
            rows = spot(band, mid)
            total = product(planes_of(left, count, every) + planes_of(own, per, rows), rights)
            first, second = total[:, :quarter], total[:, quarter:]
            kept[part, rows, :] = jnp.where(core == 0, first, second)
            sent[part, rows, :] = jnp.where(core == 0, second, first)


def block_rows(far, part, away, home, same, near, own, mate, other):
    count, mid, _ = away.shape
    per = own.shape[0]
    every = pl.ds(0, mid)
    cols = spot(part, mid)
    right = planes_of(same, per, cols) + planes_of(near, per, cols)
    right += [other.at[per + p] for p in range(per)] + [other.at[p] for p in range(per)]
    for band, left in ((1 - far, away), (far, home)):
        rows = spot(band, mid)
        lefts = planes_of(left, count, every)
        lefts += planes_of(own, per, rows) + planes_of(mate, per, rows)
        yield rows, product(lefts, right)


def away_kernel(
    away, home, same, near, own, mate, other, kept, got, straight, crossed
):
    core, far = sides()
    width = crossed.shape[1]
    for rows, total in block_rows(far, 1 - far, away, home, same, near, own, mate, other):
        first, second = total[:, :width], total[:, width:]
        straight[rows, :width] = jnp.where(core == 0, first, second).astype(BF16)
        crossed[rows, :] = jnp.where(core == 0, second, first).astype(BF16)
        straight[rows, width:] = (kept[1 - far, rows, :] + got[1 - far, rows, :]).astype(BF16)


def home_kernel(away, home, same, near, own, mate, other, kept, got, held, sent):
    core, far = sides()
    width = sent.shape[1]
    for rows, total in block_rows(far, far, away, home, same, near, own, mate, other):
        first, second = total[:, :width], total[:, width:]
        held[0, rows, :] = jnp.where(core == 0, first, second)
        held[1, rows, :] = kept[far, rows, :] + got[far, rows, :]
        sent[rows, :] = jnp.where(core == 0, second, first)


def settle_kernel(scale, kept, straight, crossed, out, cross, held, sems):
    core, _ = sides()
    width = crossed.shape[1]
    copies = []
    for i, place in enumerate((2 - 2 * core, 1)):
        held[i] = (kept[i] + straight[:, i * width : (i + 1) * width].astype(F32)) * scale
        copies.append(pltpu.make_async_copy(held.at[i], out.at[place], sems.at[i]))
        copies[i].start()
    cross[...] = crossed[...]
    for copy in copies:
        copy.wait()


def band_kernel(scale, got, cross, band, out, held, sems):
    core, _ = sides()
    held[...] = (got[...] + cross[...].astype(F32)) * scale
    copy = pltpu.make_async_copy(held, out.at[2 * core], sems.at[0])
    copy.start()
    copy.wait()


def body(ints3c, coef, tile_mask):
    blocks = lax.axis_size("blk")
    group = lax.axis_size("aux")
    mask = jnp.transpose(tile_mask, (1, 0, 2))
    ints = jnp.transpose(ints3c, (0, 2, 1, 3))
    mask, coef, ints = in_hbm(mask), in_hbm(coef), in_hbm(ints)
    per, _, rows, inner = ints.shape
    cols = coef.shape[1]
    mid, quarter = rows // 2, rows // group

    def device(b, a):
        return (b % blocks) * group + a

    members = [(b, a) for b in range(blocks) for a in range(group)]

    def moved(value, target):
        pairs = [(device(b, a), target(b, a)) for b, a in members]
        return lax.ppermute(value, ("blk", "aux"), pairs)

    def to_edge(value):
        return moved(value, lambda b, a: device(b + 1 - 2 * (a % 2), a ^ 1))

    def to_same(value):
        return moved(value, lambda b, a: device(b - 1 + 2 * (a % 2), a))

    def within(value, flip):
        return moved(value, lambda b, a: device(b, a ^ flip))

    half = jax.ShapeDtypeStruct((per, rows, cols), BF16)
    smem = pltpu.SMEM(mask.shape, mask.dtype)
    planes = pltpu.VMEM((per, rows, inner), BF16)
    own_half, coef = call(
        own_kernel,
        "own_middle",
        [HBM, HBM, HBM],
        [half, jax.ShapeDtypeStruct(coef.shape, BF16)],
        (mask, ints, coef),
        [smem, planes, pltpu.SemaphoreType.DMA((per + 2,))],
    )
    ints, own_half = lax.optimization_barrier((ints, own_half))
    ints = in_hbm(ints)
    edge_coef = to_edge(coef)
    mate_ints = in_hbm(within(ints, 1))
    same = to_same(own_half)
    near = to_edge(own_half)
    part = jax.ShapeDtypeStruct((2 * per, mid, cols), BF16)
    away, home = call(
        edge_kernel,
        "edge_half",
        [HBM, HBM, HBM, VMEM],
        [part, part],
        (mask, ints, mate_ints, edge_coef),
        [
            smem,
            pltpu.VMEM((2 * per, rows, inner), BF16),
            pltpu.SemaphoreType.DMA((2 * per + 1,)),
        ],
        cost=COSTS["edge"],
    )
    other_away = to_edge(away)
    (mate_half,) = call(
        mate_kernel,
        "mate_middle",
        [HBM, HBM, VMEM],
        [half],
        (mask, mate_ints, coef),
        [smem, planes, pltpu.SemaphoreType.DMA((per + 1,))],
        cost=COSTS["mate"],
    )

    pair = jax.ShapeDtypeStruct((2, rows, quarter), F32)
    kept, sent = call(
        diag_kernel,
        "diag",
        [VMEM] * 3,
        [pair, pair],
        (away, home, own_half),
        cost=COSTS["diag"],
    )
    got = within(sent, 1)
    late, kept = lax.optimization_barrier((home, kept))
    other_home = to_edge(late)

    shared = (away, home, same, near, own_half, mate_half)
    quarters = jax.ShapeDtypeStruct((rows, quarter), BF16)
    straight, crossed = call(
        away_kernel,
        "away",
        [VMEM] * 9,
        [jax.ShapeDtypeStruct((rows, mid), BF16), quarters],
        shared + (other_away, kept, got),
        cost=COSTS["away"],
    )
    straight = within(straight, 2)
    crossed = within(crossed, 3)
    held, sent = call(
        home_kernel,
        "home",
        [VMEM] * 9,
        [pair, jax.ShapeDtypeStruct((rows, quarter), F32)],
        shared + (other_home, kept, got),
        cost=COSTS["home"],
    )
    got = within(sent, 1)
    scale = (group * per * 3 * cols) ** (-0.5)
    whole = jax.ShapeDtypeStruct((3, rows, quarter), F32)
    band, cross = call(
        lambda *refs: settle_kernel(scale, *refs),
        "settle",
        [VMEM] * 3,
        [whole, quarters],
        (held, straight, crossed),
        [pltpu.VMEM((2, rows, quarter), F32), pltpu.SemaphoreType.DMA((2,))],
        out_specs=[HBM, VMEM],
        cost=COSTS["settle"],
    )
    (band,) = call(
        lambda *refs: band_kernel(scale, *refs),
        "band",
        [VMEM, VMEM, HBM],
        [whole],
        (got, cross, band),
        [pltpu.VMEM((rows, quarter), F32), pltpu.SemaphoreType.DMA((1,))],
        out_specs=[HBM],
        aliases={2: 0},
    )
    return jnp.transpose(band, (1, 0, 2))


COSTS = {"edge": 3e9, "diag": 1, "mate": 8e9, "away": 8e9, "home": 1, "settle": 8e9}


def solution(mesh):
    placed = (P("aux", "blk", None, None), P("blk", None), P("blk", None, None))
    return jax.shard_map(
        body, mesh=mesh, in_specs=placed, out_specs=P("blk", None, "aux"), check_vma=False
    )
```

```python
import jax
import jax.numpy as jnp
from jax import lax
from jax.experimental import pallas as pl
from jax.experimental.pallas import tpu as pltpu
from jax.sharding import PartitionSpec as P

F32 = jnp.float32
BF16 = jnp.bfloat16
LIMIT = 8 << 20
SMEM = pl.BlockSpec(memory_space=pltpu.SMEM)
VMEM = pl.BlockSpec(memory_space=pltpu.VMEM)
HBM = pl.BlockSpec(memory_space=pltpu.HBM)


def call(kernel, name, specs, outs, operands, scratch=(), cost=1, out_specs=None, aliases=None):
    return pl.pallas_call(
        kernel,
        in_specs=specs,
        out_specs=[VMEM] * len(outs) if out_specs is None else out_specs,
        out_shape=outs,
        scratch_shapes=scratch,
        input_output_aliases=aliases or {},
        compiler_params=pltpu.CompilerParams(vmem_limit_bytes=LIMIT),
        cost_estimate=pl.CostEstimate(flops=int(cost), bytes_accessed=1, transcendentals=0),
        name=name,
    )(*operands)


def in_hbm(value):
    return pltpu.with_memory_space_constraint(value, pltpu.HBM)


def dot_rows(left, right):
    return lax.dot_general(left, right, (((1,), (1,)), ((), ())), preferred_element_type=F32)


def weighted(mask_ref, k, first, plane, orbitals):
    full = jnp.dot(plane[...], orbitals[...], preferred_element_type=F32)
    step = 128
    tiles = [
        full[t * step : (t + 1) * step] * mask_ref[k, 0, first + t].astype(F32)
        for t in range(full.shape[0] // step)
    ]
    return jnp.concatenate(tiles, axis=0).astype(BF16)


def sides():
    aux = lax.axis_index("aux")
    return lax.rem(aux, 2), lax.div(aux, 2)


def own_kernel(mask, ints, orbitals, out, held, edges, mask_ref, planes, sems):
    core, _ = sides()
    per = out.shape[0]
    copies = [
        pltpu.make_async_copy(ints.at[p, 1], planes.at[p], sems.at[p]) for p in range(per)
    ]
    copies.append(pltpu.make_async_copy(orbitals, held, sems.at[per]))
    copies.append(pltpu.make_async_copy(mask, mask_ref, sems.at[per + 1]))
    fetches = [
        pltpu.make_async_copy(ints.at[p, 2 * core], edges.at[p], sems.at[per + 2 + p])
        for p in range(per)
    ]
    for i in (per, 0, per + 1, *range(1, per)):
        copies[i].start()
    for fetch in fetches:
        fetch.start()
    copies[per].wait()
    copies[per + 1].wait()
    for p in range(per):
        copies[p].wait()
        out[p] = weighted(mask_ref, 1, 0, planes.at[p], held)
    for fetch in fetches:
        fetch.wait()


def spot(part, size):
    return pl.ds(pl.multiple_of(part * size, size), size)


def edge_kernel(
    mask, own, mate, orbitals, middle, away, home, bundle, mask_ref, planes, sems
):
    core, far = sides()
    side = 2 - 2 * core
    per, rows, _ = planes.shape
    mid = rows // 2
    copies = [
        pltpu.make_async_copy(own.at[p, side], planes.at[p], sems.at[p]) for p in range(per)
    ]
    copies.append(pltpu.make_async_copy(mask, mask_ref, sems.at[per]))
    for copy in copies:
        copy.start()
    copies[per].wait()
    for p in (*range(per, 2 * per), *range(per)):
        if p < per:
            copies[p].wait()
        source = planes.at[p] if p < per else mate.at[p - per]
        for out, part in ((away, 1 - far), (home, far)):
            plane = source.at[spot(part, mid)]
            half = weighted(mask_ref, side, 2 * part, plane, orbitals)
            out[p] = half
            bundle[p, spot(part, mid), :] = half
    for p in range(per):
        bundle[2 * per + p] = middle[p]


def product(left, right):
    total = dot_rows(left[0][...], right[0][...])
    for i in range(1, len(left)):
        total += dot_rows(left[i][...], right[i][...])
    return total


def planes_of(ref, count, rows):
    return [ref.at[p, rows] for p in range(count)]


def diag_kernel(mine, theirs, out):
    core, _ = sides()
    count, rows, _ = mine.shape
    quarter = out.shape[2]
    spots = [spot(2 * h + core, quarter) for h in range(2)]
    band = rows // 2
    for r in range(2):
        lines = pl.ds(r * band, band)
        total = None
        for ref in (mine, theirs):
            for p in range(count):
                right = jnp.concatenate([ref[p, where, :] for where in spots], axis=0)
                term = dot_rows(ref[p, lines, :], right)
                total = term if total is None else total + term
        for h in range(2):
            out[h, lines, :] = total[:, h * quarter : (h + 1) * quarter]


def shared_kernel(away, home, same, near, out):
    _, far = sides()
    count, mid, _ = away.shape
    per = same.shape[0]
    cols = spot(1 - far, mid)
    rights = planes_of(same, per, cols) + planes_of(near, per, cols)
    for band, left in ((1 - far, away), (far, home)):
        out[spot(band, mid), :] = product(planes_of(left, count, pl.ds(0, mid)), rights)


def middle_part(rows, own, mate, other):
    per = own.shape[0]
    rights = [other.at[per + p] for p in range(per)] + [other.at[p] for p in range(per)]
    mates = [mate.at[2 * per + p, rows] for p in range(per)]
    return product(planes_of(own, per, rows) + mates, rights)


def away_kernel(part, own, mate, other, diag, straight, crossed):
    core, far = sides()
    width = crossed.shape[1]
    mid = 2 * width
    for r in range(2):
        rows = pl.ds(r * mid, mid)
        total = part[rows, :] + middle_part(rows, own, mate, other)
        first, second = total[:, :width], total[:, width:]
        straight[rows, :width] = jnp.where(core == 0, first, second).astype(BF16)
        crossed[rows, :] = jnp.where(core == 0, second, first).astype(BF16)
        straight[rows, width:] = diag[1 - far, rows, :].astype(BF16)


def home_kernel(away, home, same, near, own, mate, other, diag, held, sent):
    core, far = sides()
    count, mid, _ = away.shape
    per = own.shape[0]
    width = sent.shape[1]
    cols = spot(far, mid)
    rights = planes_of(same, per, cols) + planes_of(near, per, cols)
    for band, left in ((1 - far, away), (far, home)):
        rows = spot(band, mid)
        total = product(planes_of(left, count, pl.ds(0, mid)), rights)
        total += middle_part(rows, own, mate, other)
        first, second = total[:, :width], total[:, width:]
        held[0, rows, :] = jnp.where(core == 0, first, second)
        held[1, rows, :] = diag[far, rows, :]
        sent[rows, :] = jnp.where(core == 0, second, first)


def settle_kernel(scale, kept, straight, crossed, out, cross, held, sems):
    core, _ = sides()
    width = crossed.shape[1]
    copies = []
    for i, place in enumerate((2 - 2 * core, 1)):
        held[i] = (kept[i] + straight[:, i * width : (i + 1) * width].astype(F32)) * scale
        copies.append(pltpu.make_async_copy(held.at[i], out.at[place], sems.at[i]))
        copies[i].start()
    cross[...] = crossed[...]
    for copy in copies:
        copy.wait()


def band_kernel(scale, got, cross, band, out, held, sems):
    core, _ = sides()
    held[...] = (got[...] + cross[...].astype(F32)) * scale
    copy = pltpu.make_async_copy(held, out.at[2 * core], sems.at[0])
    copy.start()
    copy.wait()


def body(ints3c, coef, tile_mask):
    blocks = lax.axis_size("blk")
    group = lax.axis_size("aux")
    mask = jnp.transpose(tile_mask, (1, 0, 2))
    ints = jnp.transpose(ints3c, (0, 2, 1, 3))
    mask, coef, ints = in_hbm(mask), in_hbm(coef), in_hbm(ints)
    per, _, rows, inner = ints.shape
    cols = coef.shape[1]
    mid, quarter = rows // 2, rows // group

    def device(b, a):
        return (b % blocks) * group + a

    members = [(b, a) for b in range(blocks) for a in range(group)]

    def moved(value, target):
        pairs = [(device(b, a), target(b, a)) for b, a in members]
        return lax.ppermute(value, ("blk", "aux"), pairs)

    def to_edge(value):
        return moved(value, lambda b, a: device(b + 1 - 2 * (a % 2), a ^ 1))

    def to_same(value):
        return moved(value, lambda b, a: device(b - 1 + 2 * (a % 2), a))

    def within(value, flip):
        return moved(value, lambda b, a: device(b, a ^ flip))

    half = jax.ShapeDtypeStruct((per, rows, cols), BF16)
    smem = pltpu.SMEM(mask.shape, mask.dtype)
    planes = pltpu.VMEM((per, rows, inner), BF16)
    own_half, coef, edges = call(
        own_kernel,
        "own_middle",
        [HBM, HBM, HBM],
        [
            half,
            jax.ShapeDtypeStruct(coef.shape, BF16),
            jax.ShapeDtypeStruct((per, rows, inner), BF16),
        ],
        (mask, ints, coef),
        [smem, planes, pltpu.SemaphoreType.DMA((2 * per + 2,))],
    )
    ints, own_half = lax.optimization_barrier((ints, own_half))
    ints = in_hbm(ints)
    edge_coef = to_edge(coef)
    mate_edges = within(edges, 1)
    same = to_same(own_half)
    near = to_edge(own_half)
    part = jax.ShapeDtypeStruct((2 * per, mid, cols), BF16)
    away, home, bundle = call(
        edge_kernel,
        "edge_half",
        [HBM, HBM, VMEM, VMEM, VMEM],
        [part, part, jax.ShapeDtypeStruct((3 * per, rows, cols), BF16)],
        (mask, ints, mate_edges, edge_coef, own_half),
        [
            smem,
            planes,
            pltpu.SemaphoreType.DMA((per + 1,)),
        ],
        cost=COSTS["edge"],
    )
    other_away = to_edge(away)
    pair = jax.ShapeDtypeStruct((2, rows, quarter), F32)
    mate_bundle = within(bundle, 1)
    other_home = to_edge(home)
    (diag,) = call(
        diag_kernel, "diag", [VMEM, VMEM], [pair], (bundle, mate_bundle), cost=COSTS["diag"]
    )

    (first_part,) = call(
        shared_kernel,
        "shared",
        [VMEM] * 4,
        [jax.ShapeDtypeStruct((rows, mid), F32)],
        (away, home, same, near),
        cost=COSTS["shared"],
    )
    quarters = jax.ShapeDtypeStruct((rows, quarter), BF16)
    straight, crossed = call(
        away_kernel,
        "away",
        [VMEM] * 5,
        [jax.ShapeDtypeStruct((rows, mid), BF16), quarters],
        (first_part, own_half, mate_bundle, other_away, diag),
        cost=COSTS["away"],
    )
    straight = within(straight, 2)
    crossed = within(crossed, 3)
    held, sent = call(
        home_kernel,
        "home",
        [VMEM] * 8,
        [pair, jax.ShapeDtypeStruct((rows, quarter), F32)],
        (away, home, same, near, own_half, mate_bundle, other_home, diag),
        cost=COSTS["home"],
    )
    got = within(sent, 1)
    scale = (group * per * 3 * cols) ** (-0.5)
    whole = jax.ShapeDtypeStruct((3, rows, quarter), F32)
    band, cross = call(
        lambda *refs: settle_kernel(scale, *refs),
        "settle",
        [VMEM] * 3,
        [whole, quarters],
        (held, straight, crossed),
        [pltpu.VMEM((2, rows, quarter), F32), pltpu.SemaphoreType.DMA((2,))],
        out_specs=[HBM, VMEM],
        cost=COSTS["settle"],
    )
    (band,) = call(
        lambda *refs: band_kernel(scale, *refs),
        "band",
        [VMEM, VMEM, HBM],
        [whole],
        (got, cross, band),
        [pltpu.VMEM((rows, quarter), F32), pltpu.SemaphoreType.DMA((1,))],
        out_specs=[HBM],
        aliases={2: 0},
    )
    return jnp.transpose(band, (1, 0, 2))


COSTS = {"edge": 3e9, "diag": 1, "shared": 2e10, "away": 8e9, "home": 1, "settle": 8e9}


def solution(mesh):
    placed = (P("aux", "blk", None, None), P("blk", None), P("blk", None, None))
    return jax.shard_map(
        body, mesh=mesh, in_specs=placed, out_specs=P("blk", None, "aux"), check_vma=False
    )
```

```python
import jax
import jax.numpy as jnp
from jax import lax
from jax.experimental import pallas as pl
from jax.experimental.pallas import tpu as pltpu
from jax.sharding import PartitionSpec as P

F32 = jnp.float32
BF16 = jnp.bfloat16
LIMIT = 8 << 20
SMEM = pl.BlockSpec(memory_space=pltpu.SMEM)
VMEM = pl.BlockSpec(memory_space=pltpu.VMEM)
HBM = pl.BlockSpec(memory_space=pltpu.HBM)


def call(kernel, name, specs, outs, operands, scratch=(), cost=1, out_specs=None, aliases=None):
    return pl.pallas_call(
        kernel,
        in_specs=specs,
        out_specs=[VMEM] * len(outs) if out_specs is None else out_specs,
        out_shape=outs,
        scratch_shapes=scratch,
        input_output_aliases=aliases or {},
        compiler_params=pltpu.CompilerParams(vmem_limit_bytes=LIMIT),
        cost_estimate=pl.CostEstimate(flops=int(cost), bytes_accessed=1, transcendentals=0),
        name=name,
    )(*operands)


def in_hbm(value):
    return pltpu.with_memory_space_constraint(value, pltpu.HBM)


def dot_rows(left, right):
    return lax.dot_general(left, right, (((1,), (1,)), ((), ())), preferred_element_type=F32)


def weighted(mask_ref, k, first, plane, orbitals):
    full = jnp.dot(plane[...], orbitals[...], preferred_element_type=F32)
    step = 128
    tiles = [
        full[t * step : (t + 1) * step] * mask_ref[k, 0, first + t].astype(F32)
        for t in range(full.shape[0] // step)
    ]
    return jnp.concatenate(tiles, axis=0).astype(BF16)


def sides():
    aux = lax.axis_index("aux")
    return lax.rem(aux, 2), lax.div(aux, 2)


def own_kernel(mask, ints, orbitals, out, held, edges, mask_ref, planes, sems):
    core, _ = sides()
    per = out.shape[0]
    copies = [
        pltpu.make_async_copy(ints.at[p, 1], planes.at[p], sems.at[p]) for p in range(per)
    ]
    copies.append(pltpu.make_async_copy(orbitals, held, sems.at[per]))
    copies.append(pltpu.make_async_copy(mask, mask_ref, sems.at[per + 1]))
    fetches = [
        pltpu.make_async_copy(ints.at[p, 2 * core], edges.at[p], sems.at[per + 2 + p])
        for p in range(per)
    ]
    for i in (per, 0, per + 1, *range(1, per)):
        copies[i].start()
    for fetch in fetches:
        fetch.start()
    copies[per].wait()
    copies[per + 1].wait()
    for p in range(per):
        copies[p].wait()
        out[p] = weighted(mask_ref, 1, 0, planes.at[p], held)
    for fetch in fetches:
        fetch.wait()


def spot(part, size):
    return pl.ds(pl.multiple_of(part * size, size), size)


def edge_kernel(
    mask, own, mate, orbitals, middle, away, home, bundle, mask_ref, planes, sems
):
    core, far = sides()
    side = 2 - 2 * core
    per, rows, _ = planes.shape
    mid = rows // 2
    copies = [
        pltpu.make_async_copy(own.at[p, side], planes.at[p], sems.at[p]) for p in range(per)
    ]
    copies.append(pltpu.make_async_copy(mask, mask_ref, sems.at[per]))
    for copy in copies:
        copy.start()
    copies[per].wait()
    for p in (*range(per, 2 * per), *range(per)):
        if p < per:
            copies[p].wait()
        source = planes.at[p] if p < per else mate.at[p - per]
        for out, part in ((away, 1 - far), (home, far)):
            plane = source.at[spot(part, mid)]
            half = weighted(mask_ref, side, 2 * part, plane, orbitals)
            out[p] = half
            bundle[p, spot(part, mid), :] = half
    for p in range(per):
        bundle[2 * per + p] = middle[p]


def product(left, right):
    total = dot_rows(left[0][...], right[0][...])
    for i in range(1, len(left)):
        total += dot_rows(left[i][...], right[i][...])
    return total


def planes_of(ref, count, rows):
    return [ref.at[p, rows] for p in range(count)]


def diag_kernel(mine, theirs, out):
    core, _ = sides()
    count, rows, _ = mine.shape
    quarter = out.shape[2]
    spots = [spot(2 * h + core, quarter) for h in range(2)]
    band = rows // 2
    for r in range(2):
        lines = pl.ds(r * band, band)
        total = None
        for ref in (mine, theirs):
            for p in range(count):
                right = jnp.concatenate([ref[p, where, :] for where in spots], axis=0)
                term = dot_rows(ref[p, lines, :], right)
                total = term if total is None else total + term
        for h in range(2):
            out[h, lines, :] = total[:, h * quarter : (h + 1) * quarter]


def shared_kernel(away, home, same, near, out):
    _, far = sides()
    count, mid, _ = away.shape
    per = same.shape[0]
    cols = spot(1 - far, mid)
    rights = planes_of(same, per, cols) + planes_of(near, per, cols)
    for band, left in ((1 - far, away), (far, home)):
        out[spot(band, mid), :] = product(planes_of(left, count, pl.ds(0, mid)), rights)


def middle_part(rows, own, mate, other):
    per = own.shape[0]
    rights = [other.at[per + p] for p in range(per)] + [other.at[p] for p in range(per)]
    mates = [mate.at[2 * per + p, rows] for p in range(per)]
    return product(planes_of(own, per, rows) + mates, rights)


def away_kernel(part, own, mate, other, diag, straight, crossed):
    core, far = sides()
    width = crossed.shape[1]
    mid = 2 * width
    for r in range(2):
        rows = pl.ds(r * mid, mid)
        total = part[rows, :] + middle_part(rows, own, mate, other)
        first, second = total[:, :width], total[:, width:]
        straight[rows, :width] = jnp.where(core == 0, first, second).astype(BF16)
        crossed[rows, :] = jnp.where(core == 0, second, first).astype(BF16)
        straight[rows, width:] = diag[1 - far, rows, :].astype(BF16)


def home_kernel(away, home, same, near, own, mate, other, diag, held, sent):
    core, far = sides()
    count, mid, _ = away.shape
    per = own.shape[0]
    width = sent.shape[1]
    cols = spot(far, mid)
    rights = planes_of(same, per, cols) + planes_of(near, per, cols)
    for band, left in ((1 - far, away), (far, home)):
        rows = spot(band, mid)
        total = product(planes_of(left, count, pl.ds(0, mid)), rights)
        total += middle_part(rows, own, mate, other)
        first, second = total[:, :width], total[:, width:]
        held[0, rows, :] = jnp.where(core == 0, first, second)
        held[1, rows, :] = diag[far, rows, :]
        sent[rows, :] = jnp.where(core == 0, second, first)


def settle_kernel(scale, kept, straight, crossed, held, cross):
    width = crossed.shape[1]
    for i in range(2):
        part = straight[:, i * width : (i + 1) * width].astype(F32)
        held[i] = (kept[i] + part) * scale
    cross[...] = crossed[...]


def band_kernel(scale, got, cross, done, out, held, sems):
    core, _ = sides()
    copies = [
        pltpu.make_async_copy(source, out.at[place], sems.at[i])
        for i, (source, place) in enumerate(
            ((done.at[0], 2 - 2 * core), (done.at[1], 1), (held, 2 * core))
        )
    ]
    copies[0].start()
    copies[1].start()
    held[...] = (got[...] + cross[...].astype(F32)) * scale
    copies[2].start()
    for copy in copies:
        copy.wait()


def body(ints3c, coef, tile_mask):
    blocks = lax.axis_size("blk")
    group = lax.axis_size("aux")
    mask = jnp.transpose(tile_mask, (1, 0, 2))
    ints = jnp.transpose(ints3c, (0, 2, 1, 3))
    mask, coef, ints = in_hbm(mask), in_hbm(coef), in_hbm(ints)
    per, _, rows, inner = ints.shape
    cols = coef.shape[1]
    mid, quarter = rows // 2, rows // group

    def device(b, a):
        return (b % blocks) * group + a

    members = [(b, a) for b in range(blocks) for a in range(group)]

    def moved(value, target):
        pairs = [(device(b, a), target(b, a)) for b, a in members]
        return lax.ppermute(value, ("blk", "aux"), pairs)

    def to_edge(value):
        return moved(value, lambda b, a: device(b + 1 - 2 * (a % 2), a ^ 1))

    def to_same(value):
        return moved(value, lambda b, a: device(b - 1 + 2 * (a % 2), a))

    def within(value, flip):
        return moved(value, lambda b, a: device(b, a ^ flip))

    half = jax.ShapeDtypeStruct((per, rows, cols), BF16)
    smem = pltpu.SMEM(mask.shape, mask.dtype)
    planes = pltpu.VMEM((per, rows, inner), BF16)
    own_half, coef, edges = call(
        own_kernel,
        "own_middle",
        [HBM, HBM, HBM],
        [
            half,
            jax.ShapeDtypeStruct(coef.shape, BF16),
            jax.ShapeDtypeStruct((per, rows, inner), BF16),
        ],
        (mask, ints, coef),
        [smem, planes, pltpu.SemaphoreType.DMA((2 * per + 2,))],
    )
    ints, own_half = lax.optimization_barrier((ints, own_half))
    ints = in_hbm(ints)
    edge_coef = to_edge(coef)
    mate_edges = within(edges, 1)
    same = to_same(own_half)
    near = to_edge(own_half)
    part = jax.ShapeDtypeStruct((2 * per, mid, cols), BF16)
    away, home, bundle = call(
        edge_kernel,
        "edge_half",
        [HBM, HBM, VMEM, VMEM, VMEM],
        [part, part, jax.ShapeDtypeStruct((3 * per, rows, cols), BF16)],
        (mask, ints, mate_edges, edge_coef, own_half),
        [
            smem,
            planes,
            pltpu.SemaphoreType.DMA((per + 1,)),
        ],
        cost=COSTS["edge"],
    )
    other_away = to_edge(away)
    pair = jax.ShapeDtypeStruct((2, rows, quarter), F32)
    mate_bundle = within(bundle, 1)
    other_home = to_edge(home)
    (diag,) = call(
        diag_kernel, "diag", [VMEM, VMEM], [pair], (bundle, mate_bundle), cost=COSTS["diag"]
    )

    (first_part,) = call(
        shared_kernel,
        "shared",
        [VMEM] * 4,
        [jax.ShapeDtypeStruct((rows, mid), F32)],
        (away, home, same, near),
        cost=COSTS["shared"],
    )
    quarters = jax.ShapeDtypeStruct((rows, quarter), BF16)
    straight, crossed = call(
        away_kernel,
        "away",
        [VMEM] * 5,
        [jax.ShapeDtypeStruct((rows, mid), BF16), quarters],
        (first_part, own_half, mate_bundle, other_away, diag),
        cost=COSTS["away"],
    )
    straight = within(straight, 2)
    crossed = within(crossed, 3)
    held, sent = call(
        home_kernel,
        "home",
        [VMEM] * 8,
        [pair, jax.ShapeDtypeStruct((rows, quarter), F32)],
        (away, home, same, near, own_half, mate_bundle, other_home, diag),
        cost=COSTS["home"],
    )
    got = within(sent, 1)
    scale = (group * per * 3 * cols) ** (-0.5)
    whole = jax.ShapeDtypeStruct((3, rows, quarter), F32)
    done, cross = call(
        lambda *refs: settle_kernel(scale, *refs),
        "settle",
        [VMEM] * 3,
        [pair, quarters],
        (held, straight, crossed),
        cost=COSTS["settle"],
    )
    (band,) = call(
        lambda *refs: band_kernel(scale, *refs),
        "band",
        [VMEM] * 3,
        [whole],
        (got, cross, done),
        [pltpu.VMEM((rows, quarter), F32), pltpu.SemaphoreType.DMA((3,))],
        out_specs=[HBM],
    )
    return jnp.transpose(band, (1, 0, 2))


COSTS = {"edge": 3e9, "diag": 1, "shared": 2e10, "away": 8e9, "home": 1, "settle": 8e9}


def solution(mesh):
    placed = (P("aux", "blk", None, None), P("blk", None), P("blk", None, None))
    return jax.shard_map(
        body, mesh=mesh, in_specs=placed, out_specs=P("blk", None, "aux"), check_vma=False
    )
```

```python
import jax
import jax.numpy as jnp
from jax import lax
from jax.experimental import pallas as pl
from jax.experimental.pallas import tpu as pltpu
from jax.sharding import PartitionSpec as P

F32 = jnp.float32
BF16 = jnp.bfloat16
LIMIT = 8 << 20
SMEM = pl.BlockSpec(memory_space=pltpu.SMEM)
VMEM = pl.BlockSpec(memory_space=pltpu.VMEM)
HBM = pl.BlockSpec(memory_space=pltpu.HBM)


def call(kernel, name, specs, outs, operands, scratch=(), cost=1, out_specs=None, aliases=None):
    return pl.pallas_call(
        kernel,
        in_specs=specs,
        out_specs=[VMEM] * len(outs) if out_specs is None else out_specs,
        out_shape=outs,
        scratch_shapes=scratch,
        input_output_aliases=aliases or {},
        compiler_params=pltpu.CompilerParams(vmem_limit_bytes=LIMIT),
        cost_estimate=pl.CostEstimate(flops=int(cost), bytes_accessed=1, transcendentals=0),
        name=name,
    )(*operands)


def in_hbm(value):
    return pltpu.with_memory_space_constraint(value, pltpu.HBM)


def dot_rows(left, right):
    return lax.dot_general(left, right, (((1,), (1,)), ((), ())), preferred_element_type=F32)


def weighted(mask_ref, k, first, plane, orbitals):
    full = jnp.dot(plane[...], orbitals[...], preferred_element_type=F32)
    step = 128
    tiles = [
        full[t * step : (t + 1) * step] * mask_ref[k, 0, first + t].astype(F32)
        for t in range(full.shape[0] // step)
    ]
    return jnp.concatenate(tiles, axis=0).astype(BF16)


def sides():
    aux = lax.axis_index("aux")
    return lax.rem(aux, 2), lax.div(aux, 2)


def own_kernel(mask, ints, orbitals, out, held, edges, mask_ref, planes, sems):
    core, _ = sides()
    per = out.shape[0]
    copies = [
        pltpu.make_async_copy(ints.at[p, 1], planes.at[p], sems.at[p]) for p in range(per)
    ]
    copies.append(pltpu.make_async_copy(orbitals, held, sems.at[per]))
    copies.append(pltpu.make_async_copy(mask, mask_ref, sems.at[per + 1]))
    fetches = [
        pltpu.make_async_copy(ints.at[p, 2 * core], edges.at[p], sems.at[per + 2 + p])
        for p in range(per)
    ]
    for i in (per, 0, per + 1, *range(1, per)):
        copies[i].start()
    for fetch in fetches:
        fetch.start()
    copies[per].wait()
    copies[per + 1].wait()
    for p in range(per):
        copies[p].wait()
        out[p] = weighted(mask_ref, 1, 0, planes.at[p], held)
    for fetch in fetches:
        fetch.wait()


def spot(part, size):
    return pl.ds(pl.multiple_of(part * size, size), size)


def near_kernel(mask, ints, orbitals, out, mask_ref, planes, sems):
    core, _ = sides()
    side = 2 - 2 * core
    per = out.shape[0]
    copies = [
        pltpu.make_async_copy(ints.at[p, side], planes.at[p], sems.at[p]) for p in range(per)
    ]
    copies.append(pltpu.make_async_copy(mask, mask_ref, sems.at[per]))
    for copy in copies:
        copy.start()
    copies[per].wait()
    for p in range(per):
        copies[p].wait()
        out[p] = weighted(mask_ref, side, 0, planes.at[p], orbitals)


def edge_kernel(mask, ready, planes, orbitals, middle, away, home, bundle, mask_ref, sem):
    core, far = sides()
    side = 2 - 2 * core
    copy = pltpu.make_async_copy(mask, mask_ref, sem.at[0])
    copy.start()
    per, rows, _ = planes.shape
    mid = rows // 2
    for p in range(per):
        bundle[p] = ready[p]
        bundle[2 * per + p] = middle[p]
        for out, part in ((away, 1 - far), (home, far)):
            out[p] = ready[p, spot(part, mid), :]
    copy.wait()
    for p in range(per):
        for out, part in ((away, 1 - far), (home, far)):
            plane = planes.at[p, spot(part, mid)]
            half = weighted(mask_ref, side, 2 * part, plane, orbitals)
            out[per + p] = half
            bundle[per + p, spot(part, mid), :] = half


def product(left, right):
    total = dot_rows(left[0][...], right[0][...])
    for i in range(1, len(left)):
        total += dot_rows(left[i][...], right[i][...])
    return total


def planes_of(ref, count, rows):
    return [ref.at[p, rows] for p in range(count)]


def diag_kernel(mine, theirs, out):
    core, _ = sides()
    count, rows, _ = mine.shape
    quarter = out.shape[2]
    spots = [spot(2 * h + core, quarter) for h in range(2)]
    band = rows // 2
    for r in range(2):
        lines = pl.ds(r * band, band)
        total = None
        for ref in (mine, theirs):
            for p in range(count):
                right = jnp.concatenate([ref[p, where, :] for where in spots], axis=0)
                term = dot_rows(ref[p, lines, :], right)
                total = term if total is None else total + term
        for h in range(2):
            out[h, lines, :] = total[:, h * quarter : (h + 1) * quarter]


def shared_kernel(away, home, same, near, out):
    _, far = sides()
    count, mid, _ = away.shape
    per = same.shape[0]
    cols = spot(1 - far, mid)
    rights = planes_of(same, per, cols) + planes_of(near, per, cols)
    for band, left in ((1 - far, away), (far, home)):
        out[spot(band, mid), :] = product(planes_of(left, count, pl.ds(0, mid)), rights)


def middle_part(rows, own, mate, other):
    per = own.shape[0]
    rights = [other.at[per + p] for p in range(per)] + [other.at[p] for p in range(per)]
    mates = [mate.at[2 * per + p, rows] for p in range(per)]
    return product(planes_of(own, per, rows) + mates, rights)


def away_kernel(part, own, mate, other, diag, straight, crossed):
    core, far = sides()
    width = crossed.shape[1]
    mid = 2 * width
    for r in range(2):
        rows = pl.ds(r * mid, mid)
        total = part[rows, :] + middle_part(rows, own, mate, other)
        first, second = total[:, :width], total[:, width:]
        straight[rows, :width] = jnp.where(core == 0, first, second).astype(BF16)
        crossed[rows, :] = jnp.where(core == 0, second, first).astype(BF16)
        straight[rows, width:] = diag[1 - far, rows, :].astype(BF16)


def home_kernel(away, home, same, near, own, mate, other, diag, held, sent):
    core, far = sides()
    count, mid, _ = away.shape
    per = own.shape[0]
    width = sent.shape[1]
    cols = spot(far, mid)
    rights = planes_of(same, per, cols) + planes_of(near, per, cols)
    for band, left in ((1 - far, away), (far, home)):
        rows = spot(band, mid)
        total = product(planes_of(left, count, pl.ds(0, mid)), rights)
        total += middle_part(rows, own, mate, other)
        first, second = total[:, :width], total[:, width:]
        held[0, rows, :] = jnp.where(core == 0, first, second)
        held[1, rows, :] = diag[far, rows, :]
        sent[rows, :] = jnp.where(core == 0, second, first)


def settle_kernel(scale, kept, straight, crossed, held, cross):
    width = crossed.shape[1]
    for i in range(2):
        part = straight[:, i * width : (i + 1) * width].astype(F32)
        held[i] = (kept[i] + part) * scale
    cross[...] = crossed[...]


def band_kernel(scale, got, cross, done, out, held, sems):
    core, _ = sides()
    copies = [
        pltpu.make_async_copy(source, out.at[place], sems.at[i])
        for i, (source, place) in enumerate(
            ((done.at[0], 2 - 2 * core), (done.at[1], 1), (held, 2 * core))
        )
    ]
    copies[0].start()
    copies[1].start()
    held[...] = (got[...] + cross[...].astype(F32)) * scale
    copies[2].start()
    for copy in copies:
        copy.wait()


def body(ints3c, coef, tile_mask):
    blocks = lax.axis_size("blk")
    group = lax.axis_size("aux")
    mask = jnp.transpose(tile_mask, (1, 0, 2))
    ints = jnp.transpose(ints3c, (0, 2, 1, 3))
    mask, coef, ints = in_hbm(mask), in_hbm(coef), in_hbm(ints)
    per, _, rows, inner = ints.shape
    cols = coef.shape[1]
    mid, quarter = rows // 2, rows // group

    def device(b, a):
        return (b % blocks) * group + a

    members = [(b, a) for b in range(blocks) for a in range(group)]

    def moved(value, target):
        pairs = [(device(b, a), target(b, a)) for b, a in members]
        return lax.ppermute(value, ("blk", "aux"), pairs)

    def to_edge(value):
        return moved(value, lambda b, a: device(b + 1 - 2 * (a % 2), a ^ 1))

    def to_same(value):
        return moved(value, lambda b, a: device(b - 1 + 2 * (a % 2), a))

    def within(value, flip):
        return moved(value, lambda b, a: device(b, a ^ flip))

    half = jax.ShapeDtypeStruct((per, rows, cols), BF16)
    smem = pltpu.SMEM(mask.shape, mask.dtype)
    planes = pltpu.VMEM((per, rows, inner), BF16)
    own_half, coef, edges = call(
        own_kernel,
        "own_middle",
        [HBM, HBM, HBM],
        [
            half,
            jax.ShapeDtypeStruct(coef.shape, BF16),
            jax.ShapeDtypeStruct((per, rows, inner), BF16),
        ],
        (mask, ints, coef),
        [smem, planes, pltpu.SemaphoreType.DMA((2 * per + 2,))],
    )
    ints, own_half = lax.optimization_barrier((ints, own_half))
    ints = in_hbm(ints)
    edge_coef = to_edge(coef)
    mate_edges = within(edges, 1)
    same = to_same(own_half)
    near = to_edge(own_half)
    part = jax.ShapeDtypeStruct((2 * per, mid, cols), BF16)
    (ready,) = call(
        near_kernel,
        "near_half",
        [HBM, HBM, VMEM],
        [half],
        (mask, ints, edge_coef),
        [smem, planes, pltpu.SemaphoreType.DMA((per + 1,))],
        cost=COSTS["near"],
    )
    away, home, bundle = call(
        edge_kernel,
        "edge_half",
        [HBM] + [VMEM] * 4,
        [part, part, jax.ShapeDtypeStruct((3 * per, rows, cols), BF16)],
        (mask, ready, mate_edges, edge_coef, own_half),
        [smem, pltpu.SemaphoreType.DMA((1,))],
        cost=COSTS["edge"],
    )
    other_away = to_edge(away)
    pair = jax.ShapeDtypeStruct((2, rows, quarter), F32)
    mate_bundle = within(bundle, 1)
    other_home = to_edge(home)
    (diag,) = call(
        diag_kernel, "diag", [VMEM, VMEM], [pair], (bundle, mate_bundle), cost=COSTS["diag"]
    )

    (first_part,) = call(
        shared_kernel,
        "shared",
        [VMEM] * 4,
        [jax.ShapeDtypeStruct((rows, mid), F32)],
        (away, home, same, near),
        cost=COSTS["shared"],
    )
    quarters = jax.ShapeDtypeStruct((rows, quarter), BF16)
    straight, crossed = call(
        away_kernel,
        "away",
        [VMEM] * 5,
        [jax.ShapeDtypeStruct((rows, mid), BF16), quarters],
        (first_part, own_half, mate_bundle, other_away, diag),
        cost=COSTS["away"],
    )
    straight = within(straight, 2)
    crossed = within(crossed, 3)
    held, sent = call(
        home_kernel,
        "home",
        [VMEM] * 8,
        [pair, jax.ShapeDtypeStruct((rows, quarter), F32)],
        (away, home, same, near, own_half, mate_bundle, other_home, diag),
        cost=COSTS["home"],
    )
    got = within(sent, 1)
    scale = (group * per * 3 * cols) ** (-0.5)
    whole = jax.ShapeDtypeStruct((3, rows, quarter), F32)
    done, cross = call(
        lambda *refs: settle_kernel(scale, *refs),
        "settle",
        [VMEM] * 3,
        [pair, quarters],
        (held, straight, crossed),
        cost=COSTS["settle"],
    )
    (band,) = call(
        lambda *refs: band_kernel(scale, *refs),
        "band",
        [VMEM] * 3,
        [whole],
        (got, cross, done),
        [pltpu.VMEM((rows, quarter), F32), pltpu.SemaphoreType.DMA((3,))],
        out_specs=[HBM],
    )
    return jnp.transpose(band, (1, 0, 2))


COSTS = {"near": 1e10, "edge": 3e9, "diag": 1, "shared": 2e10, "away": 8e9, "home": 1, "settle": 8e9}


def solution(mesh):
    placed = (P("aux", "blk", None, None), P("blk", None), P("blk", None, None))
    return jax.shard_map(
        body, mesh=mesh, in_specs=placed, out_specs=P("blk", None, "aux"), check_vma=False
    )
```
